32 devices in a mesh: dp: 4 (over y, core), seq: 8 (over z, x).
Axes of the slice: x: 2, y: 2, z: 4, core: 2. Of those that a mesh axis runs over, the one named last changes fastest.
Arguments:
- block_input: bfloat16 [4, 1024, 1024], P('dp', 'seq'), may hold values from -6 to 6
- cotangent: bfloat16 [4, 1024, 1024], P('dp', 'seq'), may hold values from -6 to 6
- segment_ids: int32 [4, 1024], P('dp', 'seq'), may hold values from 0 to 3, never falling along the last dimension, each value on 1 to 512 neighbouring positions
- norm_gain: bfloat16 [1024], P(('dp', 'seq')), may hold values from 0.5 to 1.5
- in_proj: bfloat16 [1024, 3072], P(('dp', 'seq')), may hold values from -0.1875 to 0.1875
- conv_weight: bfloat16 [1024, 3], P(('dp', 'seq')), may hold values from -3.5 to 3.5
- out_proj: bfloat16 [1024, 1024], P(('dp', 'seq')), may hold values from -0.1875 to 0.1875
- ffn_gain: bfloat16 [1024], P(('dp', 'seq')), may hold values from 0.5 to 1.5
- gate_proj: bfloat16 [1024, 4608], P(('dp', 'seq')), may hold values from -0.1875 to 0.1875
- up_proj: bfloat16 [1024, 4608], P(('dp', 'seq')), may hold values from -0.1875 to 0.1875
- down_proj: bfloat16 [1024, 4608], P(('dp', 'seq')), may hold values from -0.09375 to 0.09375
Outputs:
- block_output: float32 [4, 1024, 1024], P('dp', 'seq')
- input_grad: float32 [4, 1024, 1024], P('dp', 'seq')
- norm_gain_grad: float32 [1024], P(('dp', 'seq'))
- in_proj_grad: float32 [1024, 3072], P(('dp', 'seq'))
- conv_weight_grad: float32 [1024, 3], P(('dp', 'seq'))
- out_proj_grad: float32 [1024, 1024], P(('dp', 'seq'))
- ffn_gain_grad: float32 [1024], P(('dp', 'seq'))
- gate_proj_grad: float32 [1024, 4608], P(('dp', 'seq'))
- up_proj_grad: float32 [1024, 4608], P(('dp', 'seq'))
- down_proj_grad: float32 [1024, 4608], P(('dp', 'seq'))
The draws below stay inside these ranges and needn't reach their ends.
Inputs may be any that keep to these rules, and one draw needn't show every extreme that they name: `segment_ids`: along each sequence the ids never fall; a document is a run of equal ids of 1 to 512 tokens, and some document holds exactly 512.
All inputs are finite; a program needn't handle non-finite values.
Results may differ from the reference program's by a relative error of at most 0.0091.
Values may be sent and summed in bfloat16 or wider, within the bound.
No kernel may reach another device: no remote copies, remote signals or barrier semaphores. Data moves between devices by JAX's collectives and lax.ppermute only.
A program may use at most 256 MiB of HBM per device.

```python
import math
import jax
import jax.numpy as jnp
import numpy as np
from jax import lax

D = 1024
FF = 4608
LENGTH = 1024
SEQS = 4
DOCS = 4
DOC_MOST = 512


def spiked(drawn, rng, source, target, shards_of, factor):
    def block_of(dim):
        return (jnp.arange(drawn.shape[dim]) // (drawn.shape[dim] // shards_of)).reshape((-1,) + (1,) * (drawn.ndim - 1 - dim))

    first = jax.random.permutation(rng, shards_of)[block_of(target)]
    second = (block_of(target) + shards_of // 2) % shards_of
    return jnp.where((block_of(source) == first) | (block_of(source) == second), factor * drawn, drawn)


def steps_of(rng, extent, shards, least, largest):
    gain = 1.0
    for axis_at, shards_of in shards:
        heights = jax.random.uniform(jax.random.fold_in(jax.random.fold_in(rng, 6), axis_at), (shards_of,), jnp.float32, least / len(shards), largest / len(shards))
        gain = gain * jnp.repeat(jnp.exp(heights), extent[axis_at] // shards_of).reshape((-1,) + (1,) * (len(extent) - 1 - axis_at))
    return gain


def profile(amount, total, limit, lean):
    portions = [(1 << 20) // math.isqrt(standing ** lean) + 1 for standing in range(2, amount + 1)]
    surplus, counts = total - limit - (amount - 1), [1] * (amount - 1)
    while surplus > 0:
        movable = [i for i in range(amount - 1) if counts[i] < limit]
        mass, budget = sum([portions[i] for i in movable]), surplus
        for i in movable:
            extra = min(limit - counts[i], max(1, budget * portions[i] // mass), surplus)
            counts[i] = counts[i] + extra
            surplus = surplus - extra
    return np.array([limit] + counts)


def ragged(own_key, number_of, total, reach, slope):
    if number_of == 2:
        one = jax.random.randint(own_key, (), max(1, total - reach), min(reach, total - 1) + 1)
        return jnp.stack([one, total - one])
    lengths = jnp.asarray(profile(number_of, total, reach, slope), jnp.int32)
    twos = (number_of - 1) // 2
    giver, sink = lengths[1:1 + 2 * twos:2], lengths[2:2 + 2 * twos:2]
    slack = jnp.minimum(giver - 1, reach - sink)
    passed = jax.random.randint(jax.random.fold_in(own_key, 1), (twos,), 0, 1 << 20) % (slack + 1)
    lengths = lengths.at[1:1 + 2 * twos:2].set(giver - passed).at[2:2 + 2 * twos:2].set(sink + passed)
    return lengths[jax.random.permutation(jax.random.fold_in(own_key, 2), number_of)]


def centred(key, shape, scale, reach, pieces=(), dtype=jnp.bfloat16):
    entries = scale * jax.random.normal(key, shape, jnp.float32)
    if pieces:
        entries = entries * steps_of(key, shape, pieces, -0.22, 0.18)
    return jnp.clip(entries, -reach, reach).astype(dtype)


def bell_draw_with(own_key, extent, width, limit, shards, heavy, dtype=jnp.bfloat16):
    array = width * jax.random.normal(own_key, extent, jnp.float32)
    if shards:
        array = array * steps_of(own_key, extent, shards, -0.22, 0.18)
    return jnp.clip(spiked(array, jax.random.fold_in(own_key, 3), *heavy), -limit, limit).astype(dtype)


def setup_inputs(seed: int = 0) -> dict:
    key_list = jax.random.split(jax.random.key(seed), 12)
    return {
        "block_input": centred(key_list[0], (SEQS, LENGTH, D), 1.0, 6.0, ((0, 4), (1, 8))),
        "cotangent": bell_draw_with(key_list[1], (SEQS, LENGTH, D), 1.0, 6.0, ((0, 4), (1, 8)), (1, 2, 8, 2.0)),
        "segment_ids": jax.vmap(lambda own: jnp.searchsorted(jnp.cumsum(ragged(own, DOCS, LENGTH, DOC_MOST, 1)), jnp.arange(LENGTH), side="right"))(jax.random.split(key_list[2], SEQS)).reshape((SEQS, LENGTH)).astype(jnp.int32),
        "norm_gain": jnp.clip(1.0 + 0.1 * jax.random.normal(key_list[3], (D,), jnp.float32), 0.5, 1.5).astype(jnp.bfloat16),
        "in_proj": centred(key_list[4], (D, 3 * D), D ** -0.5, 0.1875, ((0, 32),)),
        "conv_weight": centred(key_list[5], (D, 3), 3 ** -0.5, 3.5, ((0, 32),)),
        "out_proj": centred(key_list[6], (D, D), D ** -0.5, 0.1875, ((0, 32),)),
        "ffn_gain": jnp.clip(1.0 + 0.1 * jax.random.normal(key_list[7], (D,), jnp.float32), 0.5, 1.5).astype(jnp.bfloat16),
        "gate_proj": centred(key_list[8], (D, FF), D ** -0.5, 0.1875, ((0, 32),)),
        "up_proj": centred(key_list[9], (D, FF), D ** -0.5, 0.1875, ((0, 32),)),
        "down_proj": centred(key_list[10], (D, FF), FF ** -0.5, 0.09375, ((0, 32),)),
    }


EPS = 1e-05

def inverse_rms(values):
    return lax.rsqrt(lax.optimization_barrier(jnp.mean(values * values, axis=-1, keepdims=True)) + EPS)

def norm_backward(values, inverse, scaling, upstream):
    scaled = scaling * upstream
    return inverse * scaled - values * inverse ** 3 * lax.optimization_barrier(jnp.mean(scaled * values, axis=-1, keepdims=True))

def contract_rows(first_op, second_op):
    return lax.dot_general(first_op, second_op, (((0,), (0,)), ((), ())), preferred_element_type=jnp.float32)

def contract_cols(first_op, second_op):
    return lax.dot_general(first_op, second_op, (((1,), (1,)), ((), ())), preferred_element_type=jnp.float32)

def reference(block_input, cotangent, segment_ids, norm_gain, in_proj, conv_weight, out_proj, ffn_gain, gate_proj, up_proj, down_proj):
    gain_one = norm_gain.astype(jnp.float32)
    gain_two = ffn_gain.astype(jnp.float32)
    kernel = conv_weight.astype(jnp.float32)

    def one_sequence(carry, inputs):
        seq_input, seq_cotangent, seq_ids = inputs
        seq_len = seq_input.shape[0]
        seq_ids = seq_ids.astype(jnp.int32)
        incoming = seq_input.astype(jnp.float32)
        inv_one = inverse_rms(incoming)
        normed_one = (incoming * inv_one * gain_one).astype(jnp.bfloat16)
        projected = jnp.dot(normed_one, in_proj, preferred_element_type=jnp.float32)
        b_part = projected[:, :D]
        c_part = projected[:, D:2 * D]
        x_part = projected[:, 2 * D:]
        gated_in = b_part * x_part
        before_rows = jnp.concatenate([jnp.zeros((2, D), jnp.float32), gated_in], axis=0)
        seg_before = jnp.concatenate([jnp.full((2,), -1, jnp.int32), seq_ids], axis=0)
        masks_before = []
        conv_mix = jnp.zeros((seq_len, D), jnp.float32)
        for k in range(3):
            same_mask = (seg_before[k:k + seq_len] == seq_ids).astype(jnp.float32)[:, None]
            masks_before.append(same_mask)
            conv_mix = conv_mix + kernel[:, k] * before_rows[k:k + seq_len] * same_mask
        conv_out = (c_part * conv_mix).astype(jnp.bfloat16)
        hidden_res = incoming + jnp.dot(conv_out, out_proj, preferred_element_type=jnp.float32)
        inv_two = inverse_rms(hidden_res)
        normed_two = (hidden_res * inv_two * gain_two).astype(jnp.bfloat16)
        gate_pre = jnp.dot(normed_two, gate_proj, preferred_element_type=jnp.float32)
        up_pre = jnp.dot(normed_two, up_proj, preferred_element_type=jnp.float32)
        activated = (jax.nn.silu(gate_pre) * up_pre).astype(jnp.bfloat16)
        seq_output = hidden_res + contract_cols(activated, down_proj)
        d_act = jnp.dot(seq_cotangent, down_proj, preferred_element_type=jnp.float32)
        down_grad = contract_rows(seq_cotangent, activated)
        sigmoid_gate = jax.nn.sigmoid(gate_pre)
        d_gate = (d_act * up_pre * sigmoid_gate * (1.0 + gate_pre * (1.0 - sigmoid_gate))).astype(jnp.bfloat16)
        d_up = (d_act * gate_pre * sigmoid_gate).astype(jnp.bfloat16)
        gate_grad = contract_rows(normed_two, d_gate)
        up_grad = contract_rows(normed_two, d_up)
        d_norm_two = contract_cols(d_gate, gate_proj) + contract_cols(d_up, up_proj)
        gain_two_grad = lax.optimization_barrier(jnp.sum(d_norm_two * hidden_res * inv_two, axis=0))
        d_hidden = seq_cotangent.astype(jnp.float32) + norm_backward(hidden_res, inv_two, gain_two, d_norm_two)
        d_hidden_b = d_hidden.astype(jnp.bfloat16)
        d_conv_out = contract_cols(d_hidden_b, out_proj)
        out_grad = contract_rows(conv_out, d_hidden_b)
        d_mixed = d_conv_out * c_part
        d_c_part = d_conv_out * conv_mix
        after_rows = jnp.concatenate([d_mixed, jnp.zeros((2, D), jnp.float32)], axis=0)
        seg_after = jnp.concatenate([seq_ids, jnp.full((2,), -1, jnp.int32)], axis=0)
        d_gated = jnp.zeros((seq_len, D), jnp.float32)
        kernel_terms = []
        for k in range(3):
            offset = 2 - k
            same_after = (seg_after[offset:offset + seq_len] == seq_ids).astype(jnp.float32)[:, None]
            d_gated = d_gated + kernel[:, k] * after_rows[offset:offset + seq_len] * same_after
            kernel_terms.append(lax.optimization_barrier(jnp.sum(d_mixed * before_rows[k:k + seq_len] * masks_before[k], axis=0)))
        kernel_grad = jnp.stack(kernel_terms, axis=1)
        d_projected = jnp.concatenate([d_gated * x_part, d_c_part, d_gated * b_part], axis=1).astype(jnp.bfloat16)
        in_grad = contract_rows(normed_one, d_projected)
        d_norm_one = contract_cols(d_projected, in_proj)
        gain_one_grad = lax.optimization_barrier(jnp.sum(d_norm_one * incoming * inv_one, axis=0))
        seq_input_grad = d_hidden + norm_backward(incoming, inv_one, gain_one, d_norm_one)
        terms = (gain_one_grad, in_grad, kernel_grad, out_grad, gain_two_grad, gate_grad, up_grad, down_grad)
        carry = tuple((total + term for total, term in zip(carry, terms)))
        return (carry, (seq_output, seq_input_grad))
    init = (jnp.zeros((D,), jnp.float32), jnp.zeros((D, 3 * D), jnp.float32), jnp.zeros((D, 3), jnp.float32), jnp.zeros((D, D), jnp.float32), jnp.zeros((D,), jnp.float32), jnp.zeros((D, FF), jnp.float32), jnp.zeros((D, FF), jnp.float32), jnp.zeros((D, FF), jnp.float32))
    totals, stacked = lax.scan(one_sequence, init, (block_input, cotangent, segment_ids))
    return (stacked[0], stacked[1], totals[0], totals[1], totals[2], totals[3], totals[4], totals[5], totals[6], totals[7])
```

```python
import jax
import jax.numpy as jnp
from jax import lax
from jax.sharding import PartitionSpec as P

EPS = 1e-05
BF = jnp.bfloat16
F32 = jnp.float32
LANES = 128


def inverse_rms(values):
    return lax.rsqrt(jnp.mean(values * values, axis=-1, keepdims=True) + EPS)


def norm_backward(values, inverse, scaling, upstream):
    scaled = scaling * upstream
    return inverse * scaled - values * inverse**3 * jnp.mean(
        scaled * values, axis=-1, keepdims=True
    )


def dot_nn(a, b):
    return jnp.dot(a, b, preferred_element_type=F32)


def dot_tn(a, b):
    return lax.dot_general(a, b, (((0,), (0,)), ((), ())), preferred_element_type=F32)


def dot_nt(a, b):
    return lax.dot_general(a, b, (((1,), (1,)), ((), ())), preferred_element_type=F32)


def partner(value, mask):
    count = lax.axis_size("dp")
    return lax.ppermute(value, "dp", [(i, i ^ mask) for i in range(count)])


def gather_tokens(value):
    count = lax.axis_size("dp")
    blocks = [None] * count
    for m in range(0, count, 2):
        blocks[m] = value if m == 0 else partner(value, m)
    for m in range(0, count, 2):
        blocks[m + 1] = partner(blocks[m], 1)
    return jnp.concatenate(blocks, axis=0)


def reduce_tokens(partial):
    count = lax.axis_size("dp")
    rows = partial.shape[0] // count
    blocks = [partial[m * rows : (m + 1) * rows] for m in range(count)]
    sums = [None] * count
    for m in range(count - 2, -1, -2):
        other = partner(blocks[m + 1].astype(BF), 1)
        sums[m] = blocks[m] + other.astype(F32)
    total = sums[0]
    for m in range(2, count, 2):
        total = total + partner(sums[m].astype(BF), m).astype(F32)
    return total


def ring_index(offset):
    count = lax.axis_size("seq")
    half = count // 2
    me = lax.axis_index("seq")
    place = jnp.where(me % 2 == 0, me // 2, count - 1 - me // 2)
    at = (place + offset + count) % count
    return jnp.where(at < half, 2 * at, 2 * (count - 1 - at) + 1)


def ring_pairs():
    count = lax.axis_size("seq")
    order = [2 * i for i in range(count // 2)] + [count - 1 - 2 * i for i in range(count // 2)]
    forth = [(order[i], order[(i + 1) % count]) for i in range(count)]
    return forth, [(b, a) for a, b in forth]


def ring_gather(block):
    count = lax.axis_size("seq")
    forth, back = ring_pairs()
    n, r, w = block.shape
    half = n // 2
    whole = jnp.zeros((n, count, r, w), block.dtype)

    def put(whole, piece, first, offset):
        return lax.dynamic_update_slice(
            whole, piece[:, None], (first, ring_index(offset), 0, 0)
        )

    whole = put(whole, block, 0, 0)
    ahead = behind = block
    for k in range(1, count // 2):
        ahead = lax.ppermute(ahead, "seq", forth)
        behind = lax.ppermute(behind, "seq", back)
        whole = put(whole, ahead, 0, -k)
        whole = put(whole, behind, 0, k)
    ahead = lax.ppermute(ahead[:half], "seq", forth)
    behind = lax.ppermute(behind[half:], "seq", back)
    whole = put(whole, ahead, 0, -(count // 2))
    whole = put(whole, behind, half, count // 2)
    return whole.reshape(n * count * r, w)


def ring_reduce(whole, n):
    count = lax.axis_size("seq")
    forth, back = ring_pairs()
    rows, w = whole.shape
    r = rows // (n * count)
    half = n // 2
    view = whole.reshape(n, count, r, w)

    def take(offset, first, size):
        return lax.dynamic_slice(view, (first, ring_index(offset), 0, 0), (size, 1, r, w))[:, 0]

    far = count // 2
    ahead = lax.ppermute(take(far, 0, half).astype(BF), "seq", forth)
    behind = lax.ppermute(take(far, half, n - half).astype(BF), "seq", back)
    for k in range(far - 1, 0, -1):
        mine_a, mine_b = take(k, 0, n), take(-k, 0, n)
        if k == far - 1:
            mine_a = jnp.concatenate([mine_a[:half] + ahead.astype(F32), mine_a[half:]], axis=0)
            mine_b = jnp.concatenate([mine_b[:half], mine_b[half:] + behind.astype(F32)], axis=0)
        else:
            mine_a = mine_a + ahead.astype(F32)
            mine_b = mine_b + behind.astype(F32)
        ahead = lax.ppermute(mine_a.astype(BF), "seq", forth)
        behind = lax.ppermute(mine_b.astype(BF), "seq", back)
    return take(0, 0, n) + ahead.astype(F32) + behind.astype(F32)


def exchange_columns(cut):
    count = lax.axis_size("dp")
    me = lax.axis_index("dp")
    own = cut(me)
    out = jnp.zeros((count,) + own.shape, own.dtype)
    out = lax.dynamic_update_slice(out, own[None], (me, 0, 0))
    for m in range(1, count):
        got = partner(cut(me ^ m), m)
        out = lax.dynamic_update_slice(out, got[None], (me ^ m, 0, 0))
    return out


def on_device(
    block_input,
    cotangent,
    segment_ids,
    norm_gain,
    in_proj,
    conv_weight,
    out_proj,
    ffn_gain,
    gate_proj,
    up_proj,
    down_proj,
):
    _, tok, width = block_input.shape
    n = lax.axis_size("dp")
    count = lax.axis_size("seq")
    me = lax.axis_index("dp")
    r = in_proj.shape[0]
    cs = width // n
    fs = gate_proj.shape[1] // n
    wide = 3 * cs

    ids = segment_ids.reshape(tok) + 1
    ahead = lax.ppermute(ids[tok - 2 :], "seq", [(i, i + 1) for i in range(count - 1)])
    after = lax.ppermute(ids[:2], "seq", [(i + 1, i) for i in range(count - 1)])
    ext = jnp.concatenate([ahead, ids, after])
    masks = jnp.stack([ext[k : k + tok] == ids for k in (0, 1, 3, 4)], axis=1).astype(BF)
    masks = jnp.pad(masks, ((0, 0), (0, LANES - 4)))

    incoming_b = block_input.reshape(tok, width)
    upstream_b = cotangent.reshape(tok, width)

    in_view = in_proj.reshape(r, 3, n, cs)
    small = jnp.concatenate([norm_gain[:, None], ffn_gain[:, None], conv_weight], axis=1)
    small = jnp.pad(small, ((0, 0), (0, LANES - 5)))

    def cut_mixer(s):
        part = lax.dynamic_slice(in_view, (0, 0, s, 0), (r, 3, 1, cs)).reshape(r, wide)
        return jnp.concatenate([part, small], axis=1)

    def cut_ffn(s):
        return jnp.concatenate(
            [lax.dynamic_slice(v, (0, s * fs), (r, fs)) for v in (gate_proj, up_proj, down_proj)],
            axis=1,
        )

    mixer_block = exchange_columns(cut_mixer)
    out_block = out_proj.reshape(r, n, cs).transpose(1, 0, 2)
    mixer_all = ring_gather(jnp.concatenate([mixer_block, out_block], axis=2))
    tokens_all = gather_tokens(jnp.concatenate([incoming_b, masks], axis=1))
    ffn_block = exchange_columns(cut_ffn)
    gate_up = ring_gather(ffn_block[:, :, : 2 * fs])
    down_w = ring_gather(ffn_block[:, :, 2 * fs :])
    upstream_all = gather_tokens(upstream_b)

    in_w = mixer_all[:, :wide]
    small_all = mixer_all[:, wide : wide + 5].astype(F32)
    out_w = (
        mixer_all[:, wide + LANES :]
        .reshape(n, count * r, cs)
        .transpose(1, 0, 2)
        .reshape(count * r, width)
    )
    gain_one = small_all[:, 0]
    gain_two = small_all[:, 1]
    taps = lax.dynamic_slice(small_all, (me * cs, 2), (cs, 3))

    all_in = tokens_all[:, :width].astype(F32)
    hat_one = all_in * inverse_rms(all_in)
    normed_one = (hat_one * gain_one).astype(BF)
    mask_cols = tokens_all[:, width : width + 4].astype(F32).reshape(n, tok, 4)
    projected = dot_nn(normed_one, in_w)
    b_part = projected[:, :cs]
    c_part = projected[:, cs : 2 * cs]
    x_part = projected[:, 2 * cs :]
    gated = (b_part * x_part).reshape(n, tok, cs)
    prev = lax.ppermute(gated[:, tok - 2 :], "seq", [(i, i + 1) for i in range(count - 1)])
    before = jnp.concatenate([prev, gated], axis=1)
    back_two = before[:, :tok] * mask_cols[:, :, 0:1]
    back_one = before[:, 1 : tok + 1] * mask_cols[:, :, 1:2]
    conv_mix = (taps[:, 0] * back_two + taps[:, 1] * back_one + taps[:, 2] * gated).reshape(
        n * tok, cs
    )
    conv_out = (c_part * conv_mix).astype(BF)
    incoming = incoming_b.astype(F32)
    hidden_res = incoming + reduce_tokens(dot_nn(conv_out, out_w))
    inv_two = inverse_rms(hidden_res)
    normed_two = gather_tokens((hidden_res * inv_two * gain_two).astype(BF))

    pre = dot_nn(normed_two, gate_up)
    gate_pre, up_pre = pre[:, :fs], pre[:, fs:]
    sig = jax.nn.sigmoid(gate_pre)
    activated = (gate_pre * sig * up_pre).astype(BF)
    d_act = dot_nn(upstream_all, down_w)
    d_gate = (d_act * up_pre * sig * (1.0 + gate_pre * (1.0 - sig))).astype(BF)
    d_up = (d_act * gate_pre * sig).astype(BF)
    d_pre = jnp.concatenate([d_gate, d_up], axis=1)
    d_norm_two = reduce_tokens(dot_nt(d_pre, gate_up))
    gate_up_grad = dot_tn(normed_two, d_pre)
    down_grad = dot_tn(upstream_all, activated)
    block_output = hidden_res + reduce_tokens(dot_nt(activated, down_w))

    gain_two_part = jnp.sum(d_norm_two * hidden_res * inv_two, axis=0)
    d_hidden = upstream_b.astype(F32) + norm_backward(hidden_res, inv_two, gain_two, d_norm_two)
    d_hidden_all = gather_tokens(d_hidden.astype(BF))

    d_conv_out = dot_nt(d_hidden_all, out_w)
    out_grad = dot_tn(conv_out, d_hidden_all)
    d_mixed = (d_conv_out * c_part).reshape(n, tok, cs)
    d_c_part = d_conv_out * conv_mix
    nxt = lax.ppermute(d_mixed[:, :2], "seq", [(i + 1, i) for i in range(count - 1)])
    later = jnp.concatenate([d_mixed, nxt], axis=1)
    d_gated = (
        taps[:, 2] * d_mixed
        + taps[:, 1] * later[:, 1 : tok + 1] * mask_cols[:, :, 2:3]
        + taps[:, 0] * later[:, 2:] * mask_cols[:, :, 3:4]
    ).reshape(n * tok, cs)
    taps_part = jnp.stack(
        [jnp.sum(d_mixed * v, axis=(0, 1)) for v in (back_two, back_one, gated)], axis=1
    )
    d_projected = jnp.concatenate(
        [d_gated * x_part, d_c_part, d_gated * b_part], axis=1
    ).astype(BF)
    in_grad = dot_tn(normed_one, d_projected)
    d_norm_one_part = dot_nt(d_projected, in_w)
    gain_one_part = jnp.sum(d_norm_one_part * hat_one, axis=0)
    d_norm_one = reduce_tokens(d_norm_one_part)
    inv_one = inverse_rms(incoming)
    input_grad = d_hidden + norm_backward(incoming, inv_one, gain_one, d_norm_one)

    def to_owner(share, w):
        pieces = []
        for m in range(n):
            part = lax.dynamic_slice(share, (me ^ m, 0, 0), (1, r, w))[0]
            pieces.append(part if m == 0 else partner(part.astype(BF), m).astype(F32))
        return pieces

    def spread(pieces, first, w):
        out = jnp.zeros((r, n * w), F32)
        for m in range(n):
            out = lax.dynamic_update_slice(out, pieces[m][:, first : first + w], (0, (me ^ m) * w))
        return out

    gu_pieces = to_owner(ring_reduce(gate_up_grad, n), 2 * fs)
    down_pieces = to_owner(ring_reduce(down_grad, n), fs)
    gate_out = spread(gu_pieces, 0, fs)
    up_out = spread(gu_pieces, fs, fs)
    down_out = spread(down_pieces, 0, fs)

    taps_rows = lax.dynamic_update_slice(jnp.zeros((width, 3), F32), taps_part, (me * cs, 0))
    small_part = jnp.concatenate([gain_one_part[:, None], gain_two_part[:, None], taps_rows], axis=1)
    small_part = jnp.pad(small_part, ((0, 0), (0, LANES - 5)))
    out_rows = (
        out_grad.reshape(count * r, n, cs).transpose(1, 0, 2).reshape(width, cs)
    )
    mixer_share = ring_reduce(jnp.concatenate([in_grad, small_part, out_rows], axis=1), n)
    out_out = mixer_share[:, :, wide + LANES :].transpose(1, 0, 2).reshape(r, width)
    mixer_pieces = to_owner(mixer_share[:, :, : wide + LANES], wide + LANES)
    in_out = jnp.zeros((r, 3, n, cs), F32)
    for m in range(n):
        in_out = lax.dynamic_update_slice(
            in_out, mixer_pieces[m][:, :wide].reshape(r, 3, 1, cs), (0, 0, me ^ m, 0)
        )
    small_sum = sum(piece[:, wide : wide + 5] for piece in mixer_pieces)

    shape = block_input.shape
    return (
        block_output.reshape(shape),
        input_grad.reshape(shape),
        small_sum[:, 0],
        in_out.reshape(r, n * wide),
        small_sum[:, 2:5],
        out_out,
        small_sum[:, 1],
        gate_out,
        up_out,
        down_out,
    )


def solution(mesh):
    rows = P(("dp", "seq"), None)
    vector = P(("dp", "seq"))
    tokens = P("dp", "seq", None)
    return jax.shard_map(
        on_device,
        mesh=mesh,
        in_specs=(
            tokens,
            tokens,
            P("dp", "seq"),
            vector,
            rows,
            rows,
            rows,
            vector,
            rows,
            rows,
            rows,
        ),
        out_specs=(tokens, tokens, vector, rows, rows, rows, vector, rows, rows, rows),
        check_vma=False,
    )
```

```python
import jax
import jax.numpy as jnp
from jax import lax
from jax.experimental import pallas as pl
from jax.experimental.pallas import tpu as pltpu
from jax.sharding import PartitionSpec as P

EPS = 1e-05
BF = jnp.bfloat16
F32 = jnp.float32
LANES = 128


def inverse_rms(values):
    return lax.rsqrt(jnp.mean(values * values, axis=-1, keepdims=True) + EPS)


def norm_backward(values, inverse, scaling, upstream):
    scaled = scaling * upstream
    return inverse * scaled - values * inverse**3 * jnp.mean(
        scaled * values, axis=-1, keepdims=True
    )


def dot_nn(a, b):
    return jnp.dot(a, b, preferred_element_type=F32)


def dot_tn(a, b):
    return lax.dot_general(a, b, (((0,), (0,)), ((), ())), preferred_element_type=F32)


def dot_nt(a, b):
    return lax.dot_general(a, b, (((1,), (1,)), ((), ())), preferred_element_type=F32)


def partner(value, mask):
    count = lax.axis_size("dp")
    return lax.ppermute(value, "dp", [(i, i ^ mask) for i in range(count)])


def gather_tokens(value):
    count = lax.axis_size("dp")
    blocks = [None] * count
    for m in range(0, count, 2):
        blocks[m] = value if m == 0 else partner(value, m)
    for m in range(0, count, 2):
        blocks[m + 1] = partner(blocks[m], 1)
    return jnp.concatenate(blocks, axis=0)


def reduce_tokens(partial):
    count = lax.axis_size("dp")
    rows = partial.shape[0] // count
    blocks = [partial[m * rows : (m + 1) * rows] for m in range(count)]
    sums = [None] * count
    for m in range(count - 2, -1, -2):
        other = partner(blocks[m + 1].astype(BF), 1)
        sums[m] = blocks[m] + other.astype(F32)
    total = sums[0]
    for m in range(2, count, 2):
        got = partner(sums[m].astype(BF), m)
        total = total + got.astype(F32)
    return total


def ring_index(offset):
    count = lax.axis_size("seq")
    half = count // 2
    me = lax.axis_index("seq")
    place = jnp.where(me % 2 == 0, me // 2, count - 1 - me // 2)
    at = (place + offset + count) % count
    return jnp.where(at < half, 2 * at, 2 * (count - 1 - at) + 1)


def ring_pairs():
    count = lax.axis_size("seq")
    order = [2 * i for i in range(count // 2)] + [count - 1 - 2 * i for i in range(count // 2)]
    forth = [(order[i], order[(i + 1) % count]) for i in range(count)]
    return forth, [(b, a) for a, b in forth]


def ring_gather(block):
    count = lax.axis_size("seq")
    forth, back = ring_pairs()
    n, r, w = block.shape
    half = n // 2
    whole = jnp.zeros((n, count, r, w), block.dtype)

    def put(whole, piece, first, offset):
        return lax.dynamic_update_slice(
            whole, piece[:, None], (first, ring_index(offset), 0, 0)
        )

    whole = put(whole, block, 0, 0)
    ahead = behind = block
    hops = []
    for k in range(1, count // 2):
        ahead = lax.ppermute(ahead, "seq", forth)
        behind = lax.ppermute(behind, "seq", back)
        hops.append((ahead, behind))
        whole = put(whole, ahead, 0, -k)
        whole = put(whole, behind, 0, k)
    ahead = lax.ppermute(ahead[:half], "seq", forth)
    behind = lax.ppermute(behind[half:], "seq", back)
    whole = put(whole, ahead, 0, -(count // 2))
    whole = put(whole, behind, half, count // 2)
    return whole.reshape(n * count * r, w), hops


def ring_reduce(wholes, n):
    count = lax.axis_size("seq")
    forth, back = ring_pairs()
    r = wholes[0].shape[0] // (n * count)
    half = n // 2
    views = [v.reshape(n, count, r, v.shape[1]) for v in wholes]

    def take(offset, first, size):
        at = ring_index(offset)
        parts = [
            lax.dynamic_slice(v, (first, at, 0, 0), (size, 1, r, v.shape[3]))[:, 0] for v in views
        ]
        return parts[0] if len(parts) == 1 else jnp.concatenate(parts, axis=2)

    far = count // 2
    ahead = lax.ppermute(take(far, 0, half).astype(BF), "seq", forth)
    behind = lax.ppermute(take(far, half, n - half).astype(BF), "seq", back)
    for k in range(far - 1, 0, -1):
        mine_a, mine_b = take(k, 0, n), take(-k, 0, n)
        if k == far - 1:
            mine_a = jnp.concatenate([mine_a[:half] + ahead.astype(F32), mine_a[half:]], axis=0)
            mine_b = jnp.concatenate([mine_b[:half], mine_b[half:] + behind.astype(F32)], axis=0)
        else:
            mine_a = mine_a + ahead.astype(F32)
            mine_b = mine_b + behind.astype(F32)
        ahead = lax.ppermute(mine_a.astype(BF), "seq", forth)
        behind = lax.ppermute(mine_b.astype(BF), "seq", back)
    return take(0, 0, n) + ahead.astype(F32) + behind.astype(F32)


def place_call(kernel, outs, *operands):
    me = lax.axis_index("dp").astype(jnp.int32).reshape(1)
    in_specs = [pl.BlockSpec(memory_space=pltpu.SMEM)]
    in_specs += [pl.BlockSpec(memory_space=pltpu.VMEM)] * len(operands)
    return pl.pallas_call(
        kernel,
        out_shape=[jax.ShapeDtypeStruct(shape, dtype) for shape, dtype in outs],
        in_specs=in_specs,
        out_specs=[pl.BlockSpec(memory_space=pltpu.VMEM)] * len(outs),
    )(me, *operands)


def lanes(start, size):
    return pl.ds(pl.multiple_of(start, LANES), size)


def exchange(pieces):
    return [pieces[0]] + [partner(pieces[m], m) for m in range(1, len(pieces))]


def on_device(
    block_input,
    cotangent,
    segment_ids,
    norm_gain,
    in_proj,
    conv_weight,
    out_proj,
    ffn_gain,
    gate_proj,
    up_proj,
    down_proj,
):
    _, tok, width = block_input.shape
    n = lax.axis_size("dp")
    count = lax.axis_size("seq")
    me = lax.axis_index("dp")
    r = in_proj.shape[0]
    cs = width // n
    fs = gate_proj.shape[1] // n
    wide = 3 * cs

    incoming_b = block_input.reshape(tok, width)
    upstream_b = cotangent.reshape(tok, width)

    small = jnp.concatenate([norm_gain[:, None], ffn_gain[:, None], conv_weight], axis=1)
    small = jnp.pad(small, ((0, 0), (0, LANES - 5)))
    total = wide + LANES
    kinds = (gate_proj, up_proj, down_proj)
    fine = fs % LANES == 0 and cs % LANES == 0 and r % 16 == 0

    def cut_mixer(me_ref, in_ref, small_ref, *outs):
        for m in range(n):
            for t in range(3):
                at = t * width + (me_ref[0] ^ m) * cs
                outs[m][:, t * cs : (t + 1) * cs] = in_ref[:, lanes(at, cs)]
            outs[m][:, wide:] = small_ref[...]

    def lay_mixer(me_ref, *refs):
        *parts, out_ref, block_ref = refs
        for m in range(n):
            block_ref[me_ref[0] ^ m, :, :total] = parts[m][...]
            block_ref[m, :, total:] = out_ref[:, m * cs : (m + 1) * cs]

    def cut_ffn(me_ref, *refs):
        for m in range(n):
            for t in range(3):
                part = refs[t][:, lanes((me_ref[0] ^ m) * fs, fs)]
                refs[3 + m][:, t * fs : (t + 1) * fs] = part

    def lay_ffn(me_ref, *refs):
        for m in range(n):
            refs[n][me_ref[0] ^ m] = refs[m][:, : 2 * fs]
            refs[n + 1][me_ref[0] ^ m] = refs[m][:, 2 * fs :]

    def plain_cut(s):
        part = lax.dynamic_slice(in_proj.reshape(r, 3, n, cs), (0, 0, s, 0), (r, 3, 1, cs))
        return jnp.concatenate([part.reshape(r, wide), small], axis=1)

    def plain_cut_ffn(s):
        return jnp.concatenate(
            [lax.dynamic_slice(v, (0, s * fs), (r, fs)) for v in kinds], axis=1
        )

    def plain_lay(parts):
        block = jnp.zeros((n,) + parts[0].shape, BF)
        for m in range(n):
            block = lax.dynamic_update_slice(block, parts[m][None], (me ^ m, 0, 0))
        return block

    if fine:
        cuts = place_call(cut_mixer, [((r, total), BF)] * n, in_proj, small)
        (mixer_block,) = place_call(
            lay_mixer, [((n, r, total + cs), BF)], *exchange(cuts), out_proj
        )
    else:
        mixer_block = plain_lay(exchange([plain_cut(me ^ m) for m in range(n)]))
        out_block = out_proj.reshape(r, n, cs).transpose(1, 0, 2)
        mixer_block = jnp.concatenate([mixer_block, out_block], axis=2)
    mixer_all, mixer_hops = ring_gather(mixer_block)
    segment_ids, incoming_b, upstream_b, _ = lax.optimization_barrier(
        (segment_ids, incoming_b, upstream_b, mixer_block)
    )
    ids = segment_ids.reshape(tok) + 1
    ahead = lax.ppermute(ids[tok - 2 :], "seq", [(i, i + 1) for i in range(count - 1)])
    after = lax.ppermute(ids[:2], "seq", [(i + 1, i) for i in range(count - 1)])
    ext = jnp.concatenate([ahead, ids, after])
    masks = jnp.stack([ext[k : k + tok] == ids for k in (0, 1, 3, 4)], axis=1).astype(BF)
    masks = jnp.pad(masks, ((0, 0), (0, LANES - 4)))

    tokens_all = gather_tokens(jnp.concatenate([incoming_b, masks], axis=1))
    if fine:
        cuts = place_call(cut_ffn, [((r, 3 * fs), BF)] * n, *kinds)
        gate_up_block, down_block = place_call(
            lay_ffn, [((n, r, 2 * fs), BF), ((n, r, fs), BF)], *exchange(cuts)
        )
    else:
        block = plain_lay(exchange([plain_cut_ffn(me ^ m) for m in range(n)]))
        gate_up_block, down_block = block[:, :, : 2 * fs], block[:, :, 2 * fs :]
    gate_up_block, _ = lax.optimization_barrier((gate_up_block, mixer_hops[0]))
    gate_up, gate_up_hops = ring_gather(gate_up_block)
    down_block, _ = lax.optimization_barrier((down_block, gate_up_hops[1]))
    down_w, _ = ring_gather(down_block)
    upstream_all = gather_tokens(upstream_b)

    in_w = mixer_all[:, :wide]
    small_all = mixer_all[:, wide : wide + 5].astype(F32)
    out_w = (
        mixer_all[:, wide + LANES :]
        .reshape(n, count * r, cs)
        .transpose(1, 0, 2)
        .reshape(count * r, width)
    )
    gain_one = small_all[:, 0]
    gain_two = small_all[:, 1]
    taps = lax.dynamic_slice(small_all, (me * cs, 2), (cs, 3))

    all_in = tokens_all[:, :width].astype(F32)
    hat_one = all_in * inverse_rms(all_in)
    normed_one = (hat_one * gain_one).astype(BF)
    mask_cols = tokens_all[:, width : width + 4].astype(F32).reshape(n, tok, 4)
    projected = dot_nn(normed_one, in_w)
    b_part = projected[:, :cs]
    c_part = projected[:, cs : 2 * cs]
    x_part = projected[:, 2 * cs :]
    gated = (b_part * x_part).reshape(n, tok, cs)
    prev = lax.ppermute(gated[:, tok - 2 :], "seq", [(i, i + 1) for i in range(count - 1)])
    before = jnp.concatenate([prev, gated], axis=1)
    back_two = before[:, :tok] * mask_cols[:, :, 0:1]
    back_one = before[:, 1 : tok + 1] * mask_cols[:, :, 1:2]
    conv_mix = (taps[:, 0] * back_two + taps[:, 1] * back_one + taps[:, 2] * gated).reshape(
        n * tok, cs
    )
    conv_out = (c_part * conv_mix).astype(BF)
    incoming = incoming_b.astype(F32)
    hidden_res = incoming + reduce_tokens(dot_nn(conv_out, out_w))
    inv_two = inverse_rms(hidden_res)
    normed_two = gather_tokens((hidden_res * inv_two * gain_two).astype(BF))

    pre = dot_nn(normed_two, gate_up)
    gate_pre, up_pre = pre[:, :fs], pre[:, fs:]
    sig = jax.nn.sigmoid(gate_pre)
    activated = (gate_pre * sig * up_pre).astype(BF)
    down_grad = dot_tn(upstream_all, activated)
    d_act = dot_nn(upstream_all, down_w)
    d_gate = (d_act * up_pre * sig * (1.0 + gate_pre * (1.0 - sig))).astype(BF)
    d_up = (d_act * gate_pre * sig).astype(BF)
    d_pre = jnp.concatenate([d_gate, d_up], axis=1)
    d_norm_two_part = dot_nt(d_pre, gate_up)
    d_norm_two = reduce_tokens(d_norm_two_part)
    gate_up_grad = dot_tn(normed_two, d_pre)
    mixed = dot_nt(activated, down_w)
    block_output = hidden_res + reduce_tokens(mixed)

    gain_two_part = jnp.sum(d_norm_two * hidden_res * inv_two, axis=0)
    d_hidden = upstream_b.astype(F32) + norm_backward(hidden_res, inv_two, gain_two, d_norm_two)
    d_hidden_all = gather_tokens(d_hidden.astype(BF))

    d_conv_out = dot_nt(d_hidden_all, out_w)
    out_grad = dot_tn(conv_out, d_hidden_all)
    d_mixed = (d_conv_out * c_part).reshape(n, tok, cs)
    d_c_part = d_conv_out * conv_mix
    nxt = lax.ppermute(d_mixed[:, :2], "seq", [(i + 1, i) for i in range(count - 1)])
    later = jnp.concatenate([d_mixed, nxt], axis=1)
    d_gated = (
        taps[:, 2] * d_mixed
        + taps[:, 1] * later[:, 1 : tok + 1] * mask_cols[:, :, 2:3]
        + taps[:, 0] * later[:, 2:] * mask_cols[:, :, 3:4]
    ).reshape(n * tok, cs)
    taps_part = jnp.stack(
        [jnp.sum(d_mixed * v, axis=(0, 1)) for v in (back_two, back_one, gated)], axis=1
    )
    d_projected = jnp.concatenate(
        [d_gated * x_part, d_c_part, d_gated * b_part], axis=1
    ).astype(BF)
    in_grad = dot_tn(normed_one, d_projected)
    d_norm_one_part = dot_nt(d_projected, in_w)
    gain_one_part = jnp.sum(d_norm_one_part * hat_one, axis=0)
    d_norm_one = reduce_tokens(d_norm_one_part)
    inv_one = inverse_rms(incoming)
    input_grad = d_hidden + norm_backward(incoming, inv_one, gain_one, d_norm_one)

    gate_up_share = ring_reduce([gate_up_grad], n)
    down_share = ring_reduce([down_grad], n)
    taps_rows = lax.dynamic_update_slice(jnp.zeros((width, 3), F32), taps_part, (me * cs, 0))
    small_part = jnp.concatenate([gain_one_part[:, None], gain_two_part[:, None], taps_rows], axis=1)
    small_part = jnp.pad(small_part, ((0, 0), (0, LANES - 5)))
    out_rows = out_grad.reshape(count * r, n, cs).transpose(1, 0, 2).reshape(width, cs)
    mixer_share = ring_reduce([in_grad, small_part, out_rows], n)

    def part_ffn(me_ref, gu_ref, down_ref, *outs):
        for m in range(n):
            outs[m][:, : 2 * fs] = gu_ref[me_ref[0] ^ m].astype(outs[m].dtype)
            outs[m][:, 2 * fs :] = down_ref[me_ref[0] ^ m].astype(outs[m].dtype)

    def spread_ffn(me_ref, *refs):
        for m in range(n):
            for t in range(3):
                part = refs[m][:, t * fs : (t + 1) * fs].astype(F32)
                refs[n + t][:, lanes((me_ref[0] ^ m) * fs, fs)] = part

    def part_mixer(me_ref, share_ref, *outs):
        for m in range(n):
            outs[m][...] = share_ref[me_ref[0] ^ m, :, :total].astype(outs[m].dtype)
            outs[n][:, m * cs : (m + 1) * cs] = share_ref[m, :, total:]

    def spread_mixer(me_ref, *refs):
        acc = refs[0][:, wide:]
        for m in range(1, n):
            acc = acc + refs[m][:, wide:].astype(F32)
        turned = acc.T
        refs[n + 1][...] = turned[0:1]
        refs[n + 2][...] = turned[1:2]
        refs[n + 3][...] = acc[:, 2:5]
        for m in range(n):
            for t in range(3):
                at = t * width + (me_ref[0] ^ m) * cs
                refs[n][:, lanes(at, cs)] = refs[m][:, t * cs : (t + 1) * cs].astype(F32)

    if fine:
        kinds_of = lambda w: [((r, w), F32)] + [((r, w), BF)] * (n - 1)
        parts = place_call(part_ffn, kinds_of(3 * fs), gate_up_share, down_share)
        gate_out, up_out, down_out = place_call(
            spread_ffn, [((r, n * fs), F32)] * 3, *exchange(parts)
        )
        *parts, out_out = place_call(
            part_mixer, kinds_of(total) + [((r, width), F32)], mixer_share
        )
        in_out, gain_one_out, gain_two_out, taps_out = place_call(
            spread_mixer,
            [((r, n * wide), F32), ((1, r), F32), ((1, r), F32), ((r, 3), F32)],
            *exchange(parts),
        )
    else:

        def plain_parts(share):
            cut = [lax.dynamic_slice_in_dim(share, me ^ m, 1, 0)[0] for m in range(n)]
            return exchange([cut[0]] + [v.astype(BF) for v in cut[1:]])

        ffn_parts = plain_parts(jnp.concatenate([gate_up_share, down_share], axis=2))
        ffn_outs = [jnp.zeros((r, n * fs), F32) for _ in range(3)]
        mixer_parts = plain_parts(mixer_share[:, :, :total])
        in_out = jnp.zeros((r, 3, n, cs), F32)
        for m in range(n):
            for t in range(3):
                part = ffn_parts[m][:, t * fs : (t + 1) * fs].astype(F32)
                ffn_outs[t] = lax.dynamic_update_slice(ffn_outs[t], part, (0, (me ^ m) * fs))
            part = mixer_parts[m][:, :wide].reshape(r, 3, 1, cs).astype(F32)
            in_out = lax.dynamic_update_slice(in_out, part, (0, 0, me ^ m, 0))
        gate_out, up_out, down_out = ffn_outs
        in_out = in_out.reshape(r, n * wide)
        small_sum = sum(part[:, wide:].astype(F32) for part in mixer_parts)
        gain_one_out, gain_two_out, taps_out = small_sum[:, 0], small_sum[:, 1], small_sum[:, 2:5]
        out_out = mixer_share[:, :, total:].transpose(1, 0, 2).reshape(r, width)

    shape = block_input.shape
    return (
        block_output.reshape(shape),
        input_grad.reshape(shape),
        gain_one_out.reshape(r),
        in_out,
        taps_out,
        out_out,
        gain_two_out.reshape(r),
        gate_out,
        up_out,
        down_out,
    )


def solution(mesh):
    rows = P(("dp", "seq"), None)
    vector = P(("dp", "seq"))
    tokens = P("dp", "seq", None)
    return jax.shard_map(
        on_device,
        mesh=mesh,
        in_specs=(
            tokens,
            tokens,
            P("dp", "seq"),
            vector,
            rows,
            rows,
            rows,
            vector,
            rows,
            rows,
            rows,
        ),
        out_specs=(tokens, tokens, vector, rows, rows, rows, vector, rows, rows, rows),
        check_vma=False,
    )
```
